32 devices in a mesh: blk: 8 (over y, x, core), head: 4 (over z).
Axes of the slice: x: 2, y: 2, z: 4, core: 2. Of those that a mesh axis runs over, the one named last changes fastest.
Arguments:
- queries: bfloat16 [6144, 512], P('blk', 'head'), may hold values from -56 to 56
- key_states: bfloat16 [6144, 512], P('blk', 'head'), may hold values from -4 to 4
- value_states: bfloat16 [6144, 512], P('blk', 'head'), may hold values from -6 to 6
- out_grad: bfloat16 [6144, 512], P('blk', 'head'), may hold values from -6 to 6
- out_weight: bfloat16 [512, 512], P('head'), may hold values from -0.25 to 0.25
- counts: int32 [8], replicated, may hold values from 192 to 768, as said below
- patch_links: int32 [8, 3], replicated, may hold values 0 or 1
Outputs:
- attended: bfloat16 [6144, 512], P('blk', 'head')
- query_grad: bfloat16 [6144, 512], P('blk', 'head')
- key_grad: bfloat16 [6144, 512], P('blk', 'head')
- value_grad: bfloat16 [6144, 512], P('blk', 'head')
The draws below stay inside these ranges and needn't reach their ends.
Inputs may be any that keep to these rules, and one draw needn't show every extreme that they name: `counts`: some patch has all 768 points live.
All inputs are finite; a program needn't handle non-finite values.
Results may differ from the reference program's by a relative error of at most 0.02.
Values may be sent and summed in bfloat16 or wider, within the bound.
A program may use at most 64 MiB of HBM per device.

```python
import math
import jax
import jax.numpy as jnp
from jax import lax

HEADS = 8
HD = 64
P_SIZE = 768
D = 512
BLOCKS = 8
TOKENS = 6144
N_BLK = 8


def joint_fields(key):
    folded = jax.random.fold_in(key, 71)
    query_key, keys_key = jax.random.split(folded, 2)
    query_field = jax.random.truncated_normal(query_key, -4.0, 4.0, (BLOCKS, P_SIZE, D), jnp.float32)
    key_field = jax.random.truncated_normal(keys_key, -4.0, 4.0, (BLOCKS, P_SIZE, D), jnp.float32)
    return (query_field.reshape(TOKENS, D), key_field.reshape(TOKENS, D))


def draw_queries(key, part):
    return joint_fields(key)[0].astype(jnp.bfloat16)


def draw_key_states(key, part):
    return joint_fields(key)[1].astype(jnp.bfloat16)


def draw_counts(key, part):
    folded = jax.random.fold_in(key, 5)
    first_key, second_key = jax.random.split(folded)
    drawn = jax.random.randint(first_key, (BLOCKS,), P_SIZE // 4, P_SIZE + 1)
    filled = jax.random.randint(second_key, (), 0, BLOCKS)
    return jnp.where(jnp.arange(BLOCKS, dtype=jnp.int32) == filled, P_SIZE, drawn).astype(jnp.int32)


def set_ends(array, key, least, high):
    longest = array.shape.index(max(array.shape))
    spots = []
    for shift in (0, 1):
        where = [jax.random.randint(jax.random.fold_in(key, axis), (), 0, length) for axis, length in enumerate(array.shape)]
        where[longest] = (where[longest] + shift) % array.shape[longest]
        spots.append(tuple(where))
    return array.at[spots[0]].set(least).at[spots[1]].set(high)


def shard_levels(stream_key, extent, shards, smallest, top_value):
    def one(dim, blocks):
        draws = jax.random.uniform(jax.random.fold_in(jax.random.fold_in(stream_key, 6), dim), (blocks,), jnp.float32, smallest / len(shards), top_value / len(shards))
        return jnp.repeat(jnp.exp(draws), extent[dim] // blocks).reshape((-1,) + (1,) * (len(extent) - dim - 1))

    gain = one(*shards[0])
    for cut in shards[1:]:
        gain = gain * one(*cut)
    return gain


def scatter_about(rng, dims, scale, most, pieces=(), kind=jnp.bfloat16):
    result = scale * jax.random.normal(rng, dims, jnp.float32)
    if pieces:
        result = result * shard_levels(rng, dims, pieces, -0.22, 0.18)
    return jnp.clip(result, -most, most).astype(kind)


def setup_inputs(seed: int = 0) -> dict:
    arg_keys = jax.random.split(jax.random.key(seed), 8)
    queries = draw_queries(jax.random.fold_in(arg_keys[7], 71), 0)
    key_states = draw_key_states(jax.random.fold_in(arg_keys[7], 71), 0)
    value_states = scatter_about(arg_keys[2], (TOKENS, D), 1.0, 6.0, ((0, 8), (1, 4)))
    out_grad = scatter_about(arg_keys[3], (TOKENS, D), 1.0, 6.0, ((0, 8), (1, 4)))
    out_weight = scatter_about(arg_keys[4], (D, D), D ** -0.5, 0.25, ((0, 4),))
    counts = draw_counts(jax.random.fold_in(arg_keys[7], 71), 0)
    patch_links = set_ends((jax.random.randint(arg_keys[6], (BLOCKS, 3), 0, 4) < 3).astype(jnp.int32), jax.random.fold_in(arg_keys[6], 1), 0, 1)
    return dict(queries=queries, key_states=key_states, value_states=value_states, out_grad=out_grad, out_weight=out_weight, counts=counts, patch_links=patch_links)


MASKED = -1e+30

def reference(queries, key_states, value_states, out_grad, out_weight, counts, patch_links):
    cycle_size = N_BLK
    scaling = 1.0 / math.sqrt(HD)
    distances = (0, -1, 1, cycle_size // 2)
    query_stack = queries.reshape(cycle_size, P_SIZE, D)
    key_stack = key_states.reshape(cycle_size, P_SIZE, D)
    value_stack = value_states.reshape(cycle_size, P_SIZE, D)
    grad_stack = out_grad.reshape(cycle_size, P_SIZE, D)
    position = jnp.arange(P_SIZE, dtype=jnp.int32)

    def beside_all(stacked, block_index):
        gathered = []
        for distance in distances:
            owner_block = ((block_index + distance) % cycle_size).astype(jnp.int32)
            gathered.append(lax.dynamic_index_in_dim(stacked, owner_block, 0, keepdims=False))
        return jnp.concatenate(gathered)

    def one_patch(running, block_index):
        key_acc, value_acc = running
        query_block = lax.dynamic_index_in_dim(query_stack, block_index, 0, keepdims=False)
        grad_block = lax.dynamic_index_in_dim(grad_stack, block_index, 0, keepdims=False)
        seen_keys = beside_all(key_stack, block_index)
        seen_values = beside_all(value_stack, block_index)
        masks = []
        for slot_index in range(4):
            owner_block = (block_index + distances[slot_index]) % cycle_size
            usable = position < counts[owner_block]
            if slot_index > 0:
                usable = jnp.logical_and(usable, patch_links[block_index, slot_index - 1] == 1)
            masks.append(usable)
        key_live = jnp.concatenate(masks)
        query_live = (position < counts[block_index]).astype(jnp.float32)
        query_four = query_block.astype(jnp.float32).reshape(P_SIZE, HEADS, HD)
        key_four = seen_keys.astype(jnp.float32).reshape(4 * P_SIZE, HEADS, HD)
        value_four = seen_values.astype(jnp.float32).reshape(4 * P_SIZE, HEADS, HD)
        scores = jnp.einsum('qhd,khd->hqk', query_four, key_four) * scaling
        scores = jnp.where(key_live[None, None, :], scores, MASKED)
        maximum = lax.optimization_barrier(jnp.max(scores, axis=2, keepdims=True))
        powers = jnp.exp(scores - maximum)
        weights = powers / lax.optimization_barrier(jnp.sum(powers, axis=2, keepdims=True))
        masked_weights = weights * query_live[None, :, None]
        rounded = masked_weights.astype(jnp.bfloat16)
        attended_f = jnp.einsum('hqk,khd->qhd', rounded.astype(jnp.float32), value_four)
        features = attended_f.reshape(P_SIZE, D).astype(jnp.bfloat16)
        attended_block = jnp.dot(features, out_weight, preferred_element_type=jnp.float32).astype(jnp.bfloat16)
        grad_features = jnp.dot(grad_block, out_weight.T, preferred_element_type=jnp.float32).astype(jnp.bfloat16)
        grad_four = grad_features.astype(jnp.float32).reshape(P_SIZE, HEADS, HD)
        weight_grad = jnp.einsum('qhd,khd->hqk', grad_four, value_four)
        row_inner = jnp.einsum('qhd,qhd->hq', grad_four, attended_f)
        score_grad = (masked_weights * (weight_grad - row_inner[:, :, None])).astype(jnp.bfloat16)
        score_float = score_grad.astype(jnp.float32)
        query_block_grad = (jnp.einsum('hqk,khd->qhd', score_float, key_four) * scaling).reshape(P_SIZE, D).astype(jnp.bfloat16)
        key_terms = (jnp.einsum('hqk,qhd->khd', score_float, query_four) * scaling).reshape(4 * P_SIZE, D)
        value_terms = jnp.einsum('hqk,qhd->khd', rounded.astype(jnp.float32), grad_four).reshape(4 * P_SIZE, D)
        for slot_index in range(4):
            owner_block = ((block_index + distances[slot_index]) % cycle_size).astype(jnp.int32)
            key_acc = key_acc.at[owner_block].add(key_terms[slot_index * P_SIZE:(slot_index + 1) * P_SIZE])
            value_acc = value_acc.at[owner_block].add(value_terms[slot_index * P_SIZE:(slot_index + 1) * P_SIZE])
        return ((key_acc, value_acc), (attended_block, query_block_grad))
    zeros_start = jnp.zeros((cycle_size, P_SIZE, D), jnp.float32)
    finals, outputs = lax.scan(one_patch, (zeros_start, zeros_start), jnp.arange(cycle_size, dtype=jnp.int32))
    attended = outputs[0].reshape(TOKENS, D)
    query_grad = outputs[1].reshape(TOKENS, D)
    key_grad = finals[0].reshape(TOKENS, D).astype(jnp.bfloat16)
    value_grad = finals[1].reshape(TOKENS, D).astype(jnp.bfloat16)
    return (attended, query_grad, key_grad, value_grad)
```

```python
import functools
import math

import jax
import jax.numpy as jnp
from jax import lax
from jax.experimental import pallas as pl
from jax.experimental.pallas import tpu as pltpu
from jax.sharding import PartitionSpec as P

HD = 64
MASKED = -1e30
MESH = pl.DeviceIdType.MESH
F32 = jnp.float32
BF16 = jnp.bfloat16
NT = (((1,), (1,)), ((), ()))
NN = (((1,), (0,)), ((), ()))


def mm(a, b, dims=NN):
    return lax.dot_general(a, b, dims, preferred_element_type=F32)


def kernel(
    n_blk, n_head, qb,
    counts, links, q_ref, k_ref, v_ref, g_ref, w_ref,
    att_ref, dq_ref, dk_ref, dv_ref,
    kbuf, vbuf, gbuf, wbuf, fbuf, fown, kt, vt, qm, gm, gt, wts, ot, dqt, m_ref, l_ref, mslot, d_ref,
    dk_acc, dv_acc, sk, sv, rk, rv,
    kv_send, kv_recv, h_send, h_recv, r_send, r_recv,
):
    points, features = q_ref.shape
    heads = features // HD
    nq = points // qb
    scaling = 1.0 / math.sqrt(HD)
    me = lax.axis_index("blk")
    hd = lax.axis_index("head")
    half = n_blk // 2
    owners = (
        me,
        lax.rem(me + n_blk - 1, n_blk),
        lax.rem(me + 1, n_blk),
        lax.rem(me + half, n_blk),
    )
    targets = (me, owners[2], owners[1], lax.rem(me + n_blk - half, n_blk))

    barrier = pltpu.get_barrier_semaphore()
    for s in (1, 2, 3):
        pl.semaphore_signal(barrier, inc=1, device_id={"blk": owners[s]}, device_id_type=MESH)
    for r in range(1, n_head):
        pl.semaphore_signal(
            barrier, inc=1, device_id={"head": lax.rem(hd + r, n_head)}, device_id_type=MESH
        )
    pl.semaphore_wait(barrier, 3 + n_head - 1)

    def to_blk(src, dst, sends, recvs, index, target):
        return pltpu.make_async_remote_copy(
            src_ref=src, dst_ref=dst, send_sem=sends.at[index], recv_sem=recvs.at[index],
            device_id={"blk": target}, device_id_type=MESH,
        )

    def to_head(src, dst, index, target):
        return pltpu.make_async_remote_copy(
            src_ref=src, dst_ref=dst, send_sem=h_send.at[index], recv_sem=h_recv.at[index],
            device_id={"head": target}, device_id_type=MESH,
        )

    fetch = {}
    for s in (2, 1, 3):
        fetch[s] = (
            to_blk(k_ref, kbuf.at[s - 1], kv_send, kv_recv, 2 * s - 2, targets[s]),
            to_blk(v_ref, vbuf.at[s - 1], kv_send, kv_recv, 2 * s - 1, targets[s]),
        )
    gathers = []
    weights = []
    for r in range(1, n_head):
        there = lax.rem(hd + r, n_head)
        columns = pl.ds(pl.multiple_of(there * features, features), features)
        gathers.append(to_head(g_ref, gbuf.at[r - 1], r - 1, there))
        weights.append(to_head(w_ref.at[:, columns], wbuf.at[r - 1], n_head - 1 + r - 1, there))
    for s in (2, 1, 3):
        for copy in fetch[s]:
            copy.start()
    for copy in gathers + weights:
        copy.start()

    lane = lax.broadcasted_iota(jnp.int32, (1, features), 1)
    for h in range(heads):
        inside = jnp.logical_and(lane >= h * HD, lane < (h + 1) * HD)
        qm[h] = jnp.where(inside, q_ref[...].astype(F32) * scaling, 0.0).astype(BF16)
    m_ref[...] = jnp.full(m_ref.shape, MASKED, F32)
    l_ref[...] = jnp.zeros(l_ref.shape, F32)
    ot[...] = jnp.zeros(ot.shape, F32)
    dqt[...] = jnp.zeros(dqt.shape, F32)

    def forward(s, keys, values):
        kt[s] = keys[...].astype(F32).T.astype(BF16)
        vt[s] = values[...].astype(F32).T.astype(BF16)
        shown = counts[owners[s]]
        if s > 0:
            shown = shown * links[me, s - 1]
        row = lax.broadcasted_iota(jnp.int32, (points, 1), 0)
        bias = jnp.where(row < shown, 0.0, MASKED)

        for h in range(heads):

            @pl.loop(0, nq)
            def _(i):
                rows = pl.ds(pl.multiple_of(i * qb, qb), qb)
                scores = mm(keys[...], qm[h, rows, :], NT) + bias
                before = m_ref[h, i]
                top = jnp.maximum(before, jnp.max(scores, axis=0, keepdims=True))
                alpha = jnp.exp(before - top)
                powers = jnp.exp(scores - top)
                l_ref[h, i] = l_ref[h, i] * alpha + jnp.sum(powers, axis=0, keepdims=True)
                small = powers.astype(BF16)
                wts[s, h, i] = small
                ot[h, i] = ot[h, i] * alpha + mm(vt[s, h * HD:(h + 1) * HD, :], small)
                m_ref[h, i] = top
                mslot[s, h, i] = top

    forward(0, k_ref, v_ref)
    for s in (2, 1, 3):
        for copy in fetch[s]:
            copy.wait_recv()
        forward(s, kbuf.at[s - 1], vbuf.at[s - 1])

    mine = counts[me]
    for i in range(nq):
        column = lax.broadcasted_iota(jnp.int32, (1, qb), 1) + i * qb
        live = jnp.where(column < mine, 1.0, 0.0)
        for h in range(heads):
            scale = live / l_ref[h, i]
            l_ref[h, i] = scale
            ot[h, i] = ot[h, i] * scale
        fown[i * qb:(i + 1) * qb, :] = jnp.concatenate(
            [ot[h, i] for h in range(heads)], axis=0
        ).T.astype(BF16)

    for copy in gathers:
        copy.wait_recv()
    own = pl.ds(pl.multiple_of(hd * features, features), features)
    grad = mm(g_ref[...], w_ref[:, own], NT)
    for r in range(1, n_head):
        there = lax.rem(hd + n_head - r, n_head)
        columns = pl.ds(pl.multiple_of(there * features, features), features)
        grad = grad + mm(gbuf[r - 1], w_ref[:, columns], NT)
    grad = grad.astype(BF16)
    for h in range(heads):
        inside = jnp.logical_and(lane >= h * HD, lane < (h + 1) * HD)
        gm[h] = jnp.where(inside, grad.astype(F32), 0.0).astype(BF16)
    gt[...] = grad.astype(F32).T

    spread = []
    for r in range(1, n_head):
        there = lax.rem(hd + r, n_head)
        copy = to_head(fown, fbuf.at[r - 1], 2 * (n_head - 1) + r - 1, there)
        copy.start()
        spread.append(copy)

    for i in range(nq):
        for h in range(heads):
            d_ref[h, i] = jnp.sum(
                ot[h, i] * gt[h * HD:(h + 1) * HD, i * qb:(i + 1) * qb], axis=0, keepdims=True
            )

    def backward(s, values):
        for h in range(heads):

            @pl.loop(0, nq)
            def _(i):
                rows = pl.ds(pl.multiple_of(i * qb, qb), qb)
                factor = jnp.exp(mslot[s, h, i] - m_ref[h, i]) * l_ref[h, i]
                grad_rows = gm[h, rows, :]
                inner = mm(values[...], grad_rows, NT) - d_ref[h, i]
                part = wts[s, h, i].astype(F32) * factor
                score_grad = (part * inner).astype(BF16)
                value_part = mm(part.astype(BF16), grad_rows)
                key_part = mm(score_grad, qm[h, rows, :])
                dqt[h, i] += mm(kt[s, h * HD:(h + 1) * HD, :], score_grad)
                dv_acc[...] += value_part
                dk_acc[...] += key_part

    returned = []
    for s in (3, 1, 2):
        dv_acc[...] = jnp.zeros(dv_acc.shape, F32)
        dk_acc[...] = jnp.zeros(dk_acc.shape, F32)
        backward(s, vbuf.at[s - 1])
        sk[s - 1] = dk_acc[...].astype(BF16)
        sv[s - 1] = dv_acc[...].astype(BF16)
        for index, (src, dst) in enumerate(((sk, rk), (sv, rv))):
            copy = to_blk(
                src.at[s - 1], dst.at[s - 1], r_send, r_recv, 2 * s - 2 + index, owners[s]
            )
            copy.start()
            returned.append(copy)
    dv_acc[...] = jnp.zeros(dv_acc.shape, F32)
    dk_acc[...] = jnp.zeros(dk_acc.shape, F32)
    backward(0, v_ref)
    for i in range(nq):
        dq_ref[i * qb:(i + 1) * qb, :] = (
            jnp.concatenate([dqt[h, i] for h in range(heads)], axis=0).T * scaling
        ).astype(BF16)

    for copy in weights + spread:
        copy.wait_recv()
    out = mm(fown[...], w_ref[:, own])
    for r in range(1, n_head):
        out = out + mm(fbuf[r - 1], wbuf[r - 1])
    att_ref[...] = out.astype(BF16)

    for copy in returned:
        copy.wait_recv()
    dk_ref[...] = (
        dk_acc[...] + rk[0].astype(F32) + rk[1].astype(F32) + rk[2].astype(F32)
    ).astype(BF16)
    dv_ref[...] = (
        dv_acc[...] + rv[0].astype(F32) + rv[1].astype(F32) + rv[2].astype(F32)
    ).astype(BF16)

    for s in (1, 2, 3):
        for copy in fetch[s]:
            copy.wait_send()
    for copy in gathers + weights + spread + returned:
        copy.wait_send()


def body(queries, key_states, value_states, out_grad, out_weight, counts, patch_links):
    n_blk = lax.axis_size("blk")
    n_head = lax.axis_size("head")
    points, features = queries.shape
    heads = features // HD
    qb = math.gcd(points, 256)
    nq = points // qb
    rows = (points, features)
    vmem = pl.BlockSpec(memory_space=pltpu.VMEM)
    smem = pl.BlockSpec(memory_space=pltpu.SMEM)
    V = pltpu.VMEM
    dma = pltpu.SemaphoreType.DMA
    return pl.pallas_call(
        functools.partial(kernel, n_blk, n_head, qb),
        out_shape=[jax.ShapeDtypeStruct(rows, BF16)] * 4,
        in_specs=[smem, smem, vmem, vmem, vmem, vmem, vmem],
        out_specs=[vmem] * 4,
        scratch_shapes=[
            V((3,) + rows, BF16),
            V((3,) + rows, BF16),
            V((n_head - 1,) + rows, BF16),
            V((n_head - 1, features, features), BF16),
            V((n_head - 1,) + rows, BF16),
            V(rows, BF16),
            V((4, features, points), BF16),
            V((4, features, points), BF16),
            V((heads,) + rows, BF16),
            V((heads,) + rows, BF16),
            V((features, points), F32),
            V((4, heads, nq, points, qb), BF16),
            V((heads, nq, HD, qb), F32),
            V((heads, nq, HD, qb), F32),
            V((heads, nq, 1, qb), F32),
            V((heads, nq, 1, qb), F32),
            V((4, heads, nq, 1, qb), F32),
            V((heads, nq, 1, qb), F32),
            V(rows, F32),
            V(rows, F32),
            V((3,) + rows, BF16),
            V((3,) + rows, BF16),
            V((3,) + rows, BF16),
            V((3,) + rows, BF16),
            dma((6,)),
            dma((6,)),
            dma((3 * (n_head - 1),)),
            dma((3 * (n_head - 1),)),
            dma((6,)),
            dma((6,)),
        ],
        compiler_params=pltpu.CompilerParams(
            collective_id=0, has_side_effects=True, vmem_limit_bytes=56 * 1024 * 1024
        ),
    )(counts, patch_links, queries, key_states, value_states, out_grad, out_weight)


def solution(mesh):
    return jax.shard_map(
        body,
        mesh=mesh,
        in_specs=(
            P("blk", "head"),
            P("blk", "head"),
            P("blk", "head"),
            P("blk", "head"),
            P("head", None),
            P(),
            P(),
        ),
        out_specs=(P("blk", "head"), P("blk", "head"), P("blk", "head"), P("blk", "head")),
        check_vma=False,
    )
```

```python
import functools
import math

import jax
import jax.numpy as jnp
from jax import lax
from jax.experimental import pallas as pl
from jax.experimental.pallas import tpu as pltpu
from jax.sharding import PartitionSpec as P

HD = 64
MASKED = -1e30
MESH = pl.DeviceIdType.MESH
F32 = jnp.float32
BF16 = jnp.bfloat16
NT = (((1,), (1,)), ((), ()))
NN = (((1,), (0,)), ((), ()))


def mm(a, b, dims=NN):
    return lax.dot_general(a, b, dims, preferred_element_type=F32)


def kernel(
    n_blk, n_head, qb,
    counts, links, q_ref, k_ref, v_ref, g_ref, w_ref,
    att_ref, dq_ref, dk_ref, dv_ref,
    kbuf, vbuf, gbuf, pout, fbuf, fown, kt, vt, qm, gm, gt, wts, ot, dqt, m_ref, l_ref, mslot, d_ref,
    dk_acc, dv_acc, sk, sv, rk, rv,
    kv_send, kv_recv, h_send, h_recv, r_send, r_recv,
):
    points, features = q_ref.shape
    heads = features // HD
    nq = points // qb
    scaling = 1.0 / math.sqrt(HD)
    me = lax.axis_index("blk")
    hd = lax.axis_index("head")
    half = n_blk // 2
    owners = (
        me,
        lax.rem(me + n_blk - 1, n_blk),
        lax.rem(me + 1, n_blk),
        lax.rem(me + half, n_blk),
    )
    targets = (me, owners[2], owners[1], lax.rem(me + n_blk - half, n_blk))

    barrier = pltpu.get_barrier_semaphore()
    for s in (1, 2, 3):
        pl.semaphore_signal(barrier, inc=1, device_id={"blk": owners[s]}, device_id_type=MESH)
    for r in range(1, n_head):
        pl.semaphore_signal(
            barrier, inc=1, device_id={"head": lax.rem(hd + r, n_head)}, device_id_type=MESH
        )
    pl.semaphore_wait(barrier, 3 + n_head - 1)

    def to_blk(src, dst, sends, recvs, index, target):
        return pltpu.make_async_remote_copy(
            src_ref=src, dst_ref=dst, send_sem=sends.at[index], recv_sem=recvs.at[index],
            device_id={"blk": target}, device_id_type=MESH,
        )

    def to_head(src, dst, index, target):
        return pltpu.make_async_remote_copy(
            src_ref=src, dst_ref=dst, send_sem=h_send.at[index], recv_sem=h_recv.at[index],
            device_id={"head": target}, device_id_type=MESH,
        )

    fetch = {}
    for s in (2, 1, 3):
        fetch[s] = (
            to_blk(k_ref, kbuf.at[s - 1], kv_send, kv_recv, 2 * s - 2, targets[s]),
            to_blk(v_ref, vbuf.at[s - 1], kv_send, kv_recv, 2 * s - 1, targets[s]),
        )
    gathers = []
    for r in range(1, n_head):
        there = lax.rem(hd + r, n_head)
        gathers.append(to_head(g_ref, gbuf.at[r - 1], r - 1, there))
    for s in (2, 1, 3):
        for copy in fetch[s]:
            copy.start()
    for copy in gathers:
        copy.start()

    lane = lax.broadcasted_iota(jnp.int32, (1, features), 1)
    for h in range(heads):
        inside = jnp.logical_and(lane >= h * HD, lane < (h + 1) * HD)
        qm[h] = jnp.where(inside, q_ref[...].astype(F32) * scaling, 0.0).astype(BF16)
    m_ref[...] = jnp.full(m_ref.shape, MASKED, F32)
    l_ref[...] = jnp.zeros(l_ref.shape, F32)
    ot[...] = jnp.zeros(ot.shape, F32)
    dqt[...] = jnp.zeros(dqt.shape, F32)

    def forward(s, keys, values):
        kt[s] = keys[...].T
        vt[s] = values[...].T
        shown = counts[owners[s]]
        if s > 0:
            shown = shown * links[s - 1, me]
        row = lax.broadcasted_iota(jnp.int32, (points, 1), 0)
        bias = jnp.where(row < shown, 0.0, MASKED)

        for h in range(heads):

            @pl.loop(0, nq)
            def _(i):
                rows = pl.ds(pl.multiple_of(i * qb, qb), qb)
                scores = mm(keys[...], qm[h, rows, :], NT) + bias
                before = m_ref[h, i]
                top = jnp.maximum(before, jnp.max(scores, axis=0, keepdims=True))
                alpha = jnp.exp(before - top)
                powers = jnp.exp(scores - top)
                l_ref[h, i] = l_ref[h, i] * alpha + jnp.sum(powers, axis=0, keepdims=True)
                small = powers.astype(BF16)
                wts[s, h, i] = small
                ot[h, i] = ot[h, i] * alpha + mm(vt[s, h * HD:(h + 1) * HD, :], small)
                m_ref[h, i] = top
                mslot[s, h, i] = top

    forward(0, k_ref, v_ref)
    for s in (2, 1, 3):
        for copy in fetch[s]:
            copy.wait_recv()
        forward(s, kbuf.at[s - 1], vbuf.at[s - 1])

    mine = counts[me]
    for i in range(nq):
        column = lax.broadcasted_iota(jnp.int32, (1, qb), 1) + i * qb
        live = jnp.where(column < mine, 1.0, 0.0)
        for h in range(heads):
            scale = live / l_ref[h, i]
            l_ref[h, i] = scale
            ot[h, i] = ot[h, i] * scale
        fown[i * qb:(i + 1) * qb, :] = jnp.concatenate(
            [ot[h, i] for h in range(heads)], axis=0
        ).T.astype(BF16)

    spread = []
    for r in range(1, n_head):
        there = lax.rem(hd + r, n_head)
        columns = pl.ds(pl.multiple_of(there * features, features), features)
        pout[r - 1] = mm(fown[...], w_ref[:, columns]).astype(BF16)
        spread.append(to_head(pout.at[r - 1], fbuf.at[r - 1], n_head - 1 + r - 1, there))
    for copy in spread:
        copy.start()

    for copy in gathers:
        copy.wait_recv()
    own = pl.ds(pl.multiple_of(hd * features, features), features)
    grad = mm(g_ref[...], w_ref[:, own], NT)
    for r in range(1, n_head):
        there = lax.rem(hd + n_head - r, n_head)
        columns = pl.ds(pl.multiple_of(there * features, features), features)
        grad = grad + mm(gbuf[r - 1], w_ref[:, columns], NT)
    grad = grad.astype(BF16)
    for h in range(heads):
        inside = jnp.logical_and(lane >= h * HD, lane < (h + 1) * HD)
        gm[h] = jnp.where(inside, grad.astype(F32), 0.0).astype(BF16)
    gt[...] = grad.astype(F32).T

    for i in range(nq):
        for h in range(heads):
            d_ref[h, i] = jnp.sum(
                ot[h, i] * gt[h * HD:(h + 1) * HD, i * qb:(i + 1) * qb], axis=0, keepdims=True
            )

    def backward(s, values):
        for h in range(heads):

            @pl.loop(0, nq)
            def _(i):
                rows = pl.ds(pl.multiple_of(i * qb, qb), qb)
                factor = jnp.exp(mslot[s, h, i] - m_ref[h, i]) * l_ref[h, i]
                grad_rows = gm[h, rows, :]
                inner = mm(values[...], grad_rows, NT) - d_ref[h, i]
                part = wts[s, h, i].astype(F32) * factor
                score_grad = (part * inner).astype(BF16)
                value_part = mm(part.astype(BF16), grad_rows)
                key_part = mm(score_grad, qm[h, rows, :])
                dqt[h, i] += mm(kt[s, h * HD:(h + 1) * HD, :], score_grad)
                dv_acc[...] += value_part
                dk_acc[...] += key_part

    returned = []
    for s in (3, 1, 2):
        dv_acc[...] = jnp.zeros(dv_acc.shape, F32)
        dk_acc[...] = jnp.zeros(dk_acc.shape, F32)
        backward(s, vbuf.at[s - 1])
        sk[s - 1] = dk_acc[...].astype(BF16)
        sv[s - 1] = dv_acc[...].astype(BF16)
        for index, (src, dst) in enumerate(((sk, rk), (sv, rv))):
            copy = to_blk(
                src.at[s - 1], dst.at[s - 1], r_send, r_recv, 2 * s - 2 + index, owners[s]
            )
            copy.start()
            returned.append(copy)
    dv_acc[...] = jnp.zeros(dv_acc.shape, F32)
    dk_acc[...] = jnp.zeros(dk_acc.shape, F32)
    backward(0, v_ref)
    for i in range(nq):
        dq_ref[i * qb:(i + 1) * qb, :] = (
            jnp.concatenate([dqt[h, i] for h in range(heads)], axis=0).T * scaling
        ).astype(BF16)

    for copy in spread:
        copy.wait_recv()
    out = mm(fown[...], w_ref[:, own])
    for r in range(1, n_head):
        out = out + fbuf[r - 1].astype(F32)
    att_ref[...] = out.astype(BF16)

    for copy in returned:
        copy.wait_recv()
    dk_ref[...] = (
        dk_acc[...] + rk[0].astype(F32) + rk[1].astype(F32) + rk[2].astype(F32)
    ).astype(BF16)
    dv_ref[...] = (
        dv_acc[...] + rv[0].astype(F32) + rv[1].astype(F32) + rv[2].astype(F32)
    ).astype(BF16)

    for s in (1, 2, 3):
        for copy in fetch[s]:
            copy.wait_send()
    for copy in gathers + spread + returned:
        copy.wait_send()


def body(queries, key_states, value_states, out_grad, out_weight, counts, patch_links):
    n_blk = lax.axis_size("blk")
    n_head = lax.axis_size("head")
    points, features = queries.shape
    heads = features // HD
    qb = math.gcd(points, 256)
    nq = points // qb
    rows = (points, features)
    vmem = pl.BlockSpec(memory_space=pltpu.VMEM)
    smem = pl.BlockSpec(memory_space=pltpu.SMEM)
    V = pltpu.VMEM
    dma = pltpu.SemaphoreType.DMA
    return pl.pallas_call(
        functools.partial(kernel, n_blk, n_head, qb),
        out_shape=[jax.ShapeDtypeStruct(rows, BF16)] * 4,
        in_specs=[smem, smem, vmem, vmem, vmem, vmem, vmem],
        out_specs=[vmem] * 4,
        scratch_shapes=[
            V((3,) + rows, BF16),
            V((3,) + rows, BF16),
            V((n_head - 1,) + rows, BF16),
            V((n_head - 1,) + rows, BF16),
            V((n_head - 1,) + rows, BF16),
            V(rows, BF16),
            V((4, features, points), BF16),
            V((4, features, points), BF16),
            V((heads,) + rows, BF16),
            V((heads,) + rows, BF16),
            V((features, points), F32),
            V((4, heads, nq, points, qb), BF16),
            V((heads, nq, HD, qb), F32),
            V((heads, nq, HD, qb), F32),
            V((heads, nq, 1, qb), F32),
            V((heads, nq, 1, qb), F32),
            V((4, heads, nq, 1, qb), F32),
            V((heads, nq, 1, qb), F32),
            V(rows, F32),
            V(rows, F32),
            V((3,) + rows, BF16),
            V((3,) + rows, BF16),
            V((3,) + rows, BF16),
            V((3,) + rows, BF16),
            dma((6,)),
            dma((6,)),
            dma((2 * (n_head - 1),)),
            dma((2 * (n_head - 1),)),
            dma((6,)),
            dma((6,)),
        ],
        compiler_params=pltpu.CompilerParams(
            collective_id=0,
            has_side_effects=True,
            vmem_limit_bytes=56 * 1024 * 1024,
        ),
    )(counts, patch_links.T, queries, key_states, value_states, out_grad, out_weight)


def solution(mesh):
    return jax.shard_map(
        body,
        mesh=mesh,
        in_specs=(
            P("blk", "head"),
            P("blk", "head"),
            P("blk", "head"),
            P("blk", "head"),
            P("head", None),
            P(),
            P(),
        ),
        out_specs=(P("blk", "head"), P("blk", "head"), P("blk", "head"), P("blk", "head")),
        check_vma=False,
    )
```

```python
import functools
import math

import jax
import jax.numpy as jnp
from jax import lax
from jax.experimental import pallas as pl
from jax.experimental.pallas import tpu as pltpu
from jax.sharding import PartitionSpec as P

HD = 64
MASKED = -1e30
MESH = pl.DeviceIdType.MESH
F32 = jnp.float32
BF16 = jnp.bfloat16
NT = (((1,), (1,)), ((), ()))
NN = (((1,), (0,)), ((), ()))


def mm(a, b, dims=NN):
    return lax.dot_general(a, b, dims, preferred_element_type=F32)


def kernel(
    n_blk, n_head, qb,
    counts, links, q_ref, k_ref, v_ref, g_ref, w_ref,
    att_ref, dq_ref, dk_ref, dv_ref,
    kbuf, vbuf, gbuf, pout, fbuf, fown, kt, vt, qm, gm, gt, wts, ot, dqt, m_ref, l_ref, mslot, d_ref,
    dk_acc, dv_acc, sk, sv, rk, rv,
    kv_send, kv_recv, h_send, h_recv, r_send, r_recv,
):
    points, features = q_ref.shape
    heads = features // HD
    nq = points // qb
    scaling = 1.0 / math.sqrt(HD)
    me = lax.axis_index("blk")
    hd = lax.axis_index("head")
    half = n_blk // 2
    owners = (
        me,
        lax.rem(me + n_blk - 1, n_blk),
        lax.rem(me + 1, n_blk),
        lax.rem(me + half, n_blk),
    )
    targets = (me, owners[2], owners[1], lax.rem(me + n_blk - half, n_blk))

    barrier = pltpu.get_barrier_semaphore()
    for s in (1, 2, 3):
        pl.semaphore_signal(barrier, inc=1, device_id={"blk": owners[s]}, device_id_type=MESH)
    for r in range(1, n_head):
        pl.semaphore_signal(
            barrier, inc=1, device_id={"head": lax.rem(hd + r, n_head)}, device_id_type=MESH
        )
    pl.semaphore_wait(barrier, 3 + n_head - 1)

    def to_blk(src, dst, sends, recvs, index, target):
        return pltpu.make_async_remote_copy(
            src_ref=src, dst_ref=dst, send_sem=sends.at[index], recv_sem=recvs.at[index],
            device_id={"blk": target}, device_id_type=MESH,
        )

    def to_head(src, dst, index, target):
        return pltpu.make_async_remote_copy(
            src_ref=src, dst_ref=dst, send_sem=h_send.at[index], recv_sem=h_recv.at[index],
            device_id={"head": target}, device_id_type=MESH,
        )

    fetch = {}
    for s in (2, 1, 3):
        fetch[s] = (
            to_blk(k_ref, kbuf.at[s - 1], kv_send, kv_recv, 2 * s - 2, targets[s]),
            to_blk(v_ref, vbuf.at[s - 1], kv_send, kv_recv, 2 * s - 1, targets[s]),
        )
    gathers = []
    for r in range(1, n_head):
        there = lax.rem(hd + r, n_head)
        gathers.append(to_head(g_ref, gbuf.at[r - 1], r - 1, there))
    for s in (2, 1, 3):
        for copy in fetch[s]:
            copy.start()
    for copy in gathers:
        copy.start()

    lane = lax.broadcasted_iota(jnp.int32, (1, features), 1)
    for h in range(heads):
        inside = jnp.logical_and(lane >= h * HD, lane < (h + 1) * HD)
        qm[h] = jnp.where(inside, q_ref[...].astype(F32) * scaling, 0.0).astype(BF16)
    m_ref[...] = jnp.full(m_ref.shape, MASKED, F32)
    l_ref[...] = jnp.zeros(l_ref.shape, F32)
    ot[...] = jnp.zeros(ot.shape, F32)
    dqt[...] = jnp.zeros(dqt.shape, F32)

    def forward(s, keys, values):
        kt[s] = keys[...].T
        vt[s] = values[...].T
        shown = counts[owners[s]]
        if s > 0:
            shown = shown * links[s - 1, me]
        row = lax.broadcasted_iota(jnp.int32, (points, 1), 0)
        bias = jnp.where(row < shown, 0.0, MASKED)

        for h in range(heads):

            @pl.loop(0, nq)
            def _(i):
                rows = pl.ds(pl.multiple_of(i * qb, qb), qb)
                scores = mm(keys[...], qm[h, rows, :], NT) + bias
                before = m_ref[h, i]
                top = jnp.maximum(before, jnp.max(scores, axis=0, keepdims=True))
                alpha = jnp.exp(before - top)
                powers = jnp.exp(scores - top)
                l_ref[h, i] = l_ref[h, i] * alpha + jnp.sum(powers, axis=0, keepdims=True)
                small = powers.astype(BF16)
                wts[s, h, i] = small
                ot[h, i] = ot[h, i] * alpha + mm(vt[s, h * HD:(h + 1) * HD, :], small)
                m_ref[h, i] = top
                mslot[s, h, i] = top

    forward(0, k_ref, v_ref)
    for s in (2, 1, 3):
        for copy in fetch[s]:
            copy.wait_recv()
        forward(s, kbuf.at[s - 1], vbuf.at[s - 1])

    mine = counts[me]
    for i in range(nq):
        column = lax.broadcasted_iota(jnp.int32, (1, qb), 1) + i * qb
        live = jnp.where(column < mine, 1.0, 0.0)
        for h in range(heads):
            scale = live / l_ref[h, i]
            l_ref[h, i] = scale
            ot[h, i] = ot[h, i] * scale
        fown[i * qb:(i + 1) * qb, :] = jnp.concatenate(
            [ot[h, i] for h in range(heads)], axis=0
        ).T.astype(BF16)

    spread = []
    for r in range(1, n_head):
        there = lax.rem(hd + r, n_head)
        columns = pl.ds(pl.multiple_of(there * features, features), features)
        pout[r - 1] = mm(fown[...], w_ref[:, columns]).astype(BF16)
        spread.append(to_head(pout.at[r - 1], fbuf.at[r - 1], n_head - 1 + r - 1, there))
    for copy in spread:
        copy.start()

    for copy in gathers:
        copy.wait_recv()
    own = pl.ds(pl.multiple_of(hd * features, features), features)
    grad = mm(g_ref[...], w_ref[:, own], NT)
    for r in range(1, n_head):
        there = lax.rem(hd + n_head - r, n_head)
        columns = pl.ds(pl.multiple_of(there * features, features), features)
        grad = grad + mm(gbuf[r - 1], w_ref[:, columns], NT)
    grad = grad.astype(BF16)
    for h in range(heads):
        inside = jnp.logical_and(lane >= h * HD, lane < (h + 1) * HD)
        gm[h] = jnp.where(inside, grad.astype(F32), 0.0).astype(BF16)
    gt[...] = grad.astype(F32).T

    for i in range(nq):
        for h in range(heads):
            d_ref[h, i] = jnp.sum(
                ot[h, i] * gt[h * HD:(h + 1) * HD, i * qb:(i + 1) * qb], axis=0, keepdims=True
            )

    def backward(s, values):
        for h in range(heads):

            @pl.loop(0, nq)
            def _(i):
                rows = pl.ds(pl.multiple_of(i * qb, qb), qb)
                factor = jnp.exp(mslot[s, h, i] - m_ref[h, i]) * l_ref[h, i]
                grad_rows = gm[h, rows, :]
                inner = mm(values[...], grad_rows, NT) - d_ref[h, i]
                part = wts[s, h, i].astype(F32) * factor
                score_grad = (part * inner).astype(BF16)
                value_part = mm(part.astype(BF16), grad_rows)
                key_part = mm(score_grad, qm[h, rows, :])
                dqt[h, i] += mm(kt[s, h * HD:(h + 1) * HD, :], score_grad)
                dv_acc[...] += value_part
                dk_acc[...] += key_part

    returned = []
    for s in (3, 1, 2):
        dv_acc[...] = jnp.zeros(dv_acc.shape, F32)
        dk_acc[...] = jnp.zeros(dk_acc.shape, F32)
        backward(s, vbuf.at[s - 1])
        sk[s - 1] = dk_acc[...].astype(BF16)
        sv[s - 1] = dv_acc[...].astype(BF16)
        for index, (src, dst) in enumerate(((sk, rk), (sv, rv))):
            copy = to_blk(
                src.at[s - 1], dst.at[s - 1], r_send, r_recv, 2 * s - 2 + index, owners[s]
            )
            copy.start()
            returned.append(copy)
    dv_acc[...] = jnp.zeros(dv_acc.shape, F32)
    dk_acc[...] = jnp.zeros(dk_acc.shape, F32)
    backward(0, v_ref)
    for i in range(nq):
        dq_ref[i * qb:(i + 1) * qb, :] = (
            jnp.concatenate([dqt[h, i] for h in range(heads)], axis=0).T * scaling
        ).astype(BF16)

    for copy in returned:
        copy.wait_recv()
    dk_ref[...] = (
        dk_acc[...] + rk[0].astype(F32) + rk[1].astype(F32) + rk[2].astype(F32)
    ).astype(BF16)
    dv_ref[...] = (
        dv_acc[...] + rv[0].astype(F32) + rv[1].astype(F32) + rv[2].astype(F32)
    ).astype(BF16)

    for copy in spread:
        copy.wait_recv()
    out = mm(fown[...], w_ref[:, own])
    for r in range(1, n_head):
        out = out + fbuf[r - 1].astype(F32)
    att_ref[...] = out.astype(BF16)

    for s in (1, 2, 3):
        for copy in fetch[s]:
            copy.wait_send()
    for copy in gathers + spread + returned:
        copy.wait_send()


def hand_on(a, b, c, d, a_out, b_out, c_out, d_out, sems):
    copies = []
    for index, (src, dst) in enumerate(((a, a_out), (b, b_out), (c, c_out), (d, d_out))):
        copy = pltpu.make_async_copy(src, dst, sems.at[index])
        copy.start()
        copies.append(copy)
    for copy in copies:
        copy.wait()


def body(queries, key_states, value_states, out_grad, out_weight, counts, patch_links):
    n_blk = lax.axis_size("blk")
    n_head = lax.axis_size("head")
    points, features = queries.shape
    heads = features // HD
    qb = math.gcd(points, 256)
    nq = points // qb
    rows = (points, features)
    vmem = pl.BlockSpec(memory_space=pltpu.VMEM)
    smem = pl.BlockSpec(memory_space=pltpu.SMEM)
    V = pltpu.VMEM
    dma = pltpu.SemaphoreType.DMA
    results = pl.pallas_call(
        functools.partial(kernel, n_blk, n_head, qb),
        out_shape=[jax.ShapeDtypeStruct(rows, BF16)] * 4,
        in_specs=[smem, smem, vmem, vmem, vmem, vmem, vmem],
        out_specs=[vmem] * 4,
        scratch_shapes=[
            V((3,) + rows, BF16),
            V((3,) + rows, BF16),
            V((n_head - 1,) + rows, BF16),
            V((n_head - 1,) + rows, BF16),
            V((n_head - 1,) + rows, BF16),
            V(rows, BF16),
            V((4, features, points), BF16),
            V((4, features, points), BF16),
            V((heads,) + rows, BF16),
            V((heads,) + rows, BF16),
            V((features, points), F32),
            V((4, heads, nq, points, qb), BF16),
            V((heads, nq, HD, qb), F32),
            V((heads, nq, HD, qb), F32),
            V((heads, nq, 1, qb), F32),
            V((heads, nq, 1, qb), F32),
            V((4, heads, nq, 1, qb), F32),
            V((heads, nq, 1, qb), F32),
            V(rows, F32),
            V(rows, F32),
            V((3,) + rows, BF16),
            V((3,) + rows, BF16),
            V((3,) + rows, BF16),
            V((3,) + rows, BF16),
            dma((6,)),
            dma((6,)),
            dma((2 * (n_head - 1),)),
            dma((2 * (n_head - 1),)),
            dma((6,)),
            dma((6,)),
        ],
        compiler_params=pltpu.CompilerParams(
            collective_id=0,
            has_side_effects=True,
            vmem_limit_bytes=56 * 1024 * 1024,
        ),
    )(counts, patch_links.T, queries, key_states, value_states, out_grad, out_weight)
    return pl.pallas_call(
        hand_on,
        out_shape=[jax.ShapeDtypeStruct(rows, BF16)] * 4,
        in_specs=[vmem] * 4,
        out_specs=[pl.BlockSpec(memory_space=pl.ANY)] * 4,
        scratch_shapes=[dma((4,))],
    )(*results)


def solution(mesh):
    return jax.shard_map(
        body,
        mesh=mesh,
        in_specs=(
            P("blk", "head"),
            P("blk", "head"),
            P("blk", "head"),
            P("blk", "head"),
            P("head", None),
            P(),
            P(),
        ),
        out_specs=(P("blk", "head"), P("blk", "head"), P("blk", "head"), P("blk", "head")),
        check_vma=False,
    )
```
